32 devices in a mesh: group: 4 (over y, core), member: 8 (over z, x).
Axes of the slice: x: 2, y: 2, z: 4, core: 2. Of those that a mesh axis runs over, the one named last changes fastest.
Arguments:
- leaf_solution: bfloat16 [256, 64, 128], P(('group', 'member')), may hold values from -6 to 6
- leaf_panels: bfloat16 [256, 3, 4, 128, 128], P(('group', 'member')), may hold values from -0.09375 to 0.09375
- leaf_rows: int32 [256, 3, 4], P(('group', 'member')), may hold values from 0 to 31, as said below
- sep_panels: bfloat16 [32, 3, 4, 128, 128], P(('group', 'member')), may hold values from -0.25 to 0.25
- sep_rows: int32 [32, 3, 4], P(('group', 'member')), may hold values from 0 to 31, as said below
- right_sides: bfloat16 [3, 32, 64, 128], P(None, ('group', 'member')), may hold values from -6 to 6
- inverse_low: bfloat16 [32, 1024, 128], P(('group', 'member')), may hold values from -0.1875 to 0.1875
- inverse_mid: bfloat16 [32, 2048, 128], P(('group', 'member')), may hold values from -0.125 to 0.125
- inverse_top: bfloat16 [32, 4096, 128], P(('group', 'member')), may hold values from -0.09375 to 0.09375
Outputs:
- solution: bfloat16 [3, 32, 64, 128], P(None, ('group', 'member'))
The draws below stay inside these ranges and needn't reach their ends.
Inputs may be any that keep to these rules, and one draw needn't show every extreme that they name: leaf_rows[k, l, t] is below 8 * 2**l: a block of the ancestor separator at level l; indices may repeat. sep_rows[d, j, t] is below 16, 32, 32 for j = 0, 1, 2: a block of the target separator; indices may repeat.
All inputs are finite; a program needn't handle non-finite values.
Results may differ from the reference program's by a relative error of at most 0.012.
Values may be sent and summed in bfloat16 or wider, within the bound.
A program may use at most 128 MiB of HBM per device.

```python
import jax
import jax.numpy as jnp
from jax import lax

P_SIZE = 128
R = 64
NT = 4
LB = 8
SEP_BLOCKS = 8
DEV_ALL = 32


def block_indices(key, count, limits):
    raw = jax.random.randint(key, (count, 3, NT), 0, 4 * SEP_BLOCKS, dtype=jnp.int32)
    return raw % jnp.array(limits, dtype=jnp.int32)[None, :, None]


def draw_leaf_rows(key, part):
    return block_indices(jax.random.fold_in(key, 11), DEV_ALL * LB, [SEP_BLOCKS, 2 * SEP_BLOCKS, 4 * SEP_BLOCKS])


def draw_sep_rows(key, part):
    return block_indices(jax.random.fold_in(key, 23), DEV_ALL, [2 * SEP_BLOCKS, 4 * SEP_BLOCKS, 4 * SEP_BLOCKS])


def block_scale(key, shape, split, smallest, top_value):
    def one(axis_at, shards_of):
        draws = jax.random.uniform(jax.random.fold_in(jax.random.fold_in(key, 6), axis_at), (shards_of,), jnp.float32, smallest / len(split), top_value / len(split))
        return jnp.repeat(jnp.exp(draws), shape[axis_at] // shards_of).reshape((-1,) + (1,) * (len(shape) - axis_at - 1))

    gain = one(*split[0])
    for cut in split[1:]:
        gain = gain * one(*cut)
    return gain


def bell_draw(rng, extent, width, bound, cuts=(), kind=jnp.bfloat16):
    values = jax.random.normal(rng, extent, jnp.float32) * width
    if len(cuts) > 0:
        values = block_scale(rng, extent, cuts, -0.22, 0.18) * values
    return jnp.clip(values, min=-bound, max=bound).astype(kind)


def setup_inputs(seed: int = 0) -> dict:
    arg_keys = jax.random.split(jax.random.key(seed), 10)
    leaf_solution = bell_draw(arg_keys[0], (DEV_ALL * LB, R, P_SIZE), 1.0, 6.0, ((0, 32),))
    leaf_panels = bell_draw(arg_keys[1], (DEV_ALL * LB, 3, NT, P_SIZE, P_SIZE), (P_SIZE * LB * NT) ** -0.5, 0.09375, ((0, 32),))
    leaf_rows = draw_leaf_rows(jax.random.fold_in(arg_keys[9], 71), 0)
    sep_panels = bell_draw(arg_keys[3], (DEV_ALL, 3, NT, P_SIZE, P_SIZE), (P_SIZE * NT) ** -0.5, 0.25, ((0, 32),))
    sep_rows = draw_sep_rows(jax.random.fold_in(arg_keys[9], 71), 0)
    right_sides = bell_draw(arg_keys[5], (3, DEV_ALL, R, P_SIZE), 1.0, 6.0, ((1, 32),))
    inverse_low = bell_draw(arg_keys[6], (DEV_ALL, SEP_BLOCKS * P_SIZE, P_SIZE), (SEP_BLOCKS * P_SIZE) ** -0.5, 0.1875, ((0, 32),))
    inverse_mid = bell_draw(arg_keys[7], (DEV_ALL, 2 * SEP_BLOCKS * P_SIZE, P_SIZE), (2 * SEP_BLOCKS * P_SIZE) ** -0.5, 0.125, ((0, 32),))
    inverse_top = bell_draw(arg_keys[8], (DEV_ALL, 4 * SEP_BLOCKS * P_SIZE, P_SIZE), (4 * SEP_BLOCKS * P_SIZE) ** -0.5, 0.09375, ((0, 32),))
    return dict(leaf_solution=leaf_solution, leaf_panels=leaf_panels, leaf_rows=leaf_rows, sep_panels=sep_panels, sep_rows=sep_rows, right_sides=right_sides, inverse_low=inverse_low, inverse_mid=inverse_mid, inverse_top=inverse_top)


def leaf_terms(leaf_solution, leaf_panels, leaf_rows):
    total = jnp.zeros((3, DEV_ALL, R, P_SIZE), jnp.float32)

    def one(index, total):
        device = index.astype(jnp.int32)
        values = lax.dynamic_slice_in_dim(leaf_solution, device * LB, LB, 0).astype(jnp.float32)
        panels = lax.dynamic_slice_in_dim(leaf_panels, device * LB, LB, 0).astype(jnp.float32)
        rows = lax.dynamic_slice_in_dim(leaf_rows, device * LB, LB, 0)
        terms = jnp.einsum("brp,bltpq->bltrq", values, panels)
        for level in range(3):
            span = SEP_BLOCKS * 2 ** level
            target = (device // span) * span + rows[:, level, :]
            total = total.at[level, target.reshape(-1)].add(terms[:, level].reshape(-1, R, P_SIZE))
        return total

    return lax.fori_loop(0, DEV_ALL, one, total)


def sep_terms(values, panels, rows, target_level):
    span = SEP_BLOCKS * 2 ** target_level
    terms = jnp.einsum("drp,dtpq->dtrq", values.astype(jnp.float32), panels.astype(jnp.float32))
    base = (jnp.arange(DEV_ALL, dtype=jnp.int32) // span) * span
    target = base[:, None] + rows
    total = jnp.zeros((DEV_ALL, R, P_SIZE), jnp.float32)
    return total.at[target.reshape(-1)].add(terms.reshape(-1, R, P_SIZE))


def settle(resid, inverse, level):
    span = SEP_BLOCKS * 2 ** level
    seps = resid.reshape(DEV_ALL // span, span, R, P_SIZE).transpose(0, 2, 1, 3).reshape(DEV_ALL // span, R, span * P_SIZE)

    def one(device):
        return jnp.dot(seps[device // span], inverse[device], preferred_element_type=jnp.float32)

    return lax.map(one, jnp.arange(DEV_ALL, dtype=jnp.int32)).astype(jnp.bfloat16)


def reference(leaf_solution, leaf_panels, leaf_rows, sep_panels, sep_rows, right_sides, inverse_low, inverse_mid, inverse_top):
    leaf = leaf_terms(leaf_solution, leaf_panels, leaf_rows)
    resid = (right_sides[0].astype(jnp.float32) - leaf[0]).astype(jnp.bfloat16)
    first = settle(resid, inverse_low, 0)
    low_mid = sep_terms(first, sep_panels[:, 0], sep_rows[:, 0], 1)
    low_top = sep_terms(first, sep_panels[:, 1], sep_rows[:, 1], 2)
    resid = (right_sides[1].astype(jnp.float32) - (leaf[1] + low_mid)).astype(jnp.bfloat16)
    second = settle(resid, inverse_mid, 1)
    mid_top = sep_terms(second, sep_panels[:, 2], sep_rows[:, 2], 2)
    resid = (right_sides[2].astype(jnp.float32) - (leaf[2] + low_top + mid_top)).astype(jnp.bfloat16)
    third = settle(resid, inverse_top, 2)
    return jnp.stack([first, second, third])
```

```python
import functools

import jax
import jax.numpy as jnp
from jax import lax
from jax.experimental import pallas as pl
from jax.experimental.pallas import tpu as pltpu
from jax.sharding import PartitionSpec as P

MESH = pl.DeviceIdType.MESH
LEVELS = 3


def leaf_kernel(members, rows_ref, values_ref, panels_ref, out_ref, total_ref):
    block = pl.program_id(0)
    terms_each = panels_ref.shape[2]

    @pl.when(block == 0)
    def _():
        total_ref[...] = jnp.zeros_like(total_ref)

    value = values_ref[0]
    for level in range(LEVELS):
        base = members * (2**level - 1)
        for t in range(terms_each):
            term = jnp.dot(value, panels_ref[0, level, t], preferred_element_type=jnp.float32)
            where = base + rows_ref[(block * LEVELS + level) * terms_each + t]
            total_ref[where] = total_ref[where] + term

    @pl.when(block == pl.num_programs(0) - 1)
    def _():
        out_ref[...] = total_ref[...].astype(out_ref.dtype)


def leaf_parts(members, rows, values, panels):
    blocks, levels, terms_each, width, _ = panels.shape
    height = values.shape[1]
    slots = members * (2**LEVELS - 1)
    return pl.pallas_call(
        functools.partial(leaf_kernel, members),
        grid=(blocks,),
        out_shape=jax.ShapeDtypeStruct((slots, height, width), jnp.bfloat16),
        in_specs=[
            pl.BlockSpec(memory_space=pltpu.SMEM),
            pl.BlockSpec((1, height, width), lambda b: (b, 0, 0)),
            pl.BlockSpec((1, levels, terms_each, width, width), lambda b: (b, 0, 0, 0, 0)),
        ],
        out_specs=pl.BlockSpec((slots, height, width), lambda b: (0, 0, 0)),
        scratch_shapes=[pltpu.VMEM((slots, height, width), jnp.float32)],
        name="leaf_parts",
    )(rows.reshape(-1), values, panels)


def solve_kernel(
    members,
    rows_ref,
    leaf_ref,
    sides_ref,
    panels_hbm,
    low_hbm,
    mid_hbm,
    top_hbm,
    out_ref,
    sends,
    parts,
    whole,
    terms,
    panels,
    low,
    mid,
    top,
    local_sem,
    part_send,
    part_recv,
    whole_send,
    whole_recv,
):
    group, member = (lax.axis_index("group"), lax.axis_index("member"))
    inverses = (low, mid, top)
    loads = [
        pltpu.make_async_copy(source, target, local_sem.at[i])
        for i, (source, target) in enumerate(
            ((low_hbm, low), (panels_hbm, panels), (mid_hbm, mid), (top_hbm, top))
        )
    ]

    def place(level):
        count = 2**level
        first_group = group - lax.rem(group, count)
        mine = (group - first_group) * members + member
        return first_group, mine, members * count, members * (count - 1)

    def device(first_group, block):
        return (first_group + lax.div(block, members), lax.rem(block, members))

    def part_copy(level, source, peer, slot):
        first_group, mine, n, base = place(level)
        return pltpu.make_async_remote_copy(
            src_ref=source.at[base + peer],
            dst_ref=parts.at[base + slot],
            send_sem=part_send.at[base + peer],
            recv_sem=part_recv.at[base + slot],
            device_id=device(first_group, peer),
            device_id_type=MESH,
        )

    def whole_copy(level, peer, slot):
        first_group, mine, n, base = place(level)
        return pltpu.make_async_remote_copy(
            src_ref=whole.at[base + mine],
            dst_ref=whole.at[base + slot],
            send_sem=whole_send.at[base + peer],
            recv_sem=whole_recv.at[base + slot],
            device_id=device(first_group, peer),
            device_id_type=MESH,
        )

    def settle(level, source):
        _, mine, n, base = place(level)

        def send(k, _):
            part_copy(level, source, lax.rem(mine + k, n), mine).start()
            return 0

        lax.fori_loop(1, n, send, 0)

        def add(k, total):
            peer = lax.rem(mine + k, n)
            part_copy(level, source, peer, peer).wait_recv()
            return total + parts[base + peer].astype(jnp.float32)

        total = lax.fori_loop(1, n, add, source[base + mine].astype(jnp.float32))
        whole[base + mine] = (sides_ref[level].astype(jnp.float32) - total).astype(jnp.bfloat16)

        def tell(k, _):
            whole_copy(level, lax.rem(mine + k, n), mine).start()
            return 0

        lax.fori_loop(1, n, tell, 0)

        def hear(k, _):
            peer = lax.rem(mine + k, n)
            whole_copy(level, peer, peer).wait_recv()
            return 0

        lax.fori_loop(1, n, hear, 0)
        inverse = inverses[level]
        width = inverse.shape[1]
        chunk = members

        def multiply(i, total):
            start = i * chunk
            pieces = [whole[base + start + c] for c in range(chunk)]
            rows = inverse[pl.ds(pl.multiple_of(start * width, chunk * width), chunk * width), :]
            return total + jnp.dot(
                jnp.concatenate(pieces, axis=1), rows, preferred_element_type=jnp.float32
            )

        total = lax.fori_loop(0, n // chunk, multiply, jnp.zeros(out_ref.shape[1:], jnp.float32))
        value = total.astype(jnp.bfloat16)
        out_ref[level] = value
        return value

    def scatter(level, sources):
        _, mine, n, base = place(level)
        each = rows_ref.shape[1]
        named = [
            (slot * each + t, rows_ref[j, t]) for slot, j in sources for t in range(each)
        ]

        def fill(q, _):
            total = leaf_ref[base + q].astype(jnp.float32)
            for index, row in named:
                total = total + terms[index] * (row == q).astype(jnp.float32)
            sends[base + q] = total.astype(jnp.bfloat16)
            return 0

        lax.fori_loop(0, n, fill, 0)

    def drain(level, source):
        _, mine, n, base = place(level)

        def one(k, _):
            peer = lax.rem(mine + k, n)
            part_copy(level, source, peer, mine).wait_send()
            whole_copy(level, peer, mine).wait_send()
            return 0

        lax.fori_loop(1, n, one, 0)

    def products(value, slot, j):
        each = panels.shape[1]
        for t in range(each):
            terms[slot * each + t] = jnp.dot(
                value, panels[j, t], preferred_element_type=jnp.float32
            )

    for load in loads:
        load.start()
    first_group, mine, n, base = place(LEVELS - 1)
    barrier = pltpu.get_barrier_semaphore()

    def greet(k, _):
        pl.semaphore_signal(
            barrier,
            inc=1,
            device_id=device(first_group, lax.rem(mine + k, n)),
            device_id_type=MESH,
        )
        return 0

    lax.fori_loop(1, n, greet, 0)
    pl.semaphore_wait(barrier, n - 1)
    for load in loads:
        load.wait()

    first = settle(0, leaf_ref)
    products(first, 0, 0)
    products(first, 1, 1)
    scatter(1, [(0, 0)])
    second = settle(1, sends)
    products(second, 2, 2)
    scatter(2, [(1, 1), (2, 2)])
    settle(2, sends)
    drain(0, leaf_ref)
    drain(1, sends)
    drain(2, sends)


def on_device(
    leaf_solution,
    leaf_panels,
    leaf_rows,
    sep_panels,
    sep_rows,
    right_sides,
    inverse_low,
    inverse_mid,
    inverse_top,
):
    members = lax.axis_size("member")
    height, width = (leaf_solution.shape[1], leaf_solution.shape[2])
    slots = members * (2**LEVELS - 1)
    leaf = leaf_parts(members, leaf_rows, leaf_solution, leaf_panels)
    vmem = pl.BlockSpec(memory_space=pltpu.VMEM)
    hbm = pl.BlockSpec(memory_space=pl.ANY)
    each = sep_panels.shape[2]
    out = pl.pallas_call(
        functools.partial(solve_kernel, members),
        out_shape=jax.ShapeDtypeStruct((LEVELS, height, width), jnp.bfloat16),
        in_specs=[pl.BlockSpec(memory_space=pltpu.SMEM), vmem, vmem, hbm, hbm, hbm, hbm],
        out_specs=vmem,
        scratch_shapes=[
            pltpu.VMEM((slots, height, width), jnp.bfloat16),
            pltpu.VMEM((slots, height, width), jnp.bfloat16),
            pltpu.VMEM((slots, height, width), jnp.bfloat16),
            pltpu.VMEM((LEVELS * each, height, width), jnp.float32),
            pltpu.VMEM(sep_panels.shape[1:], jnp.bfloat16),
            pltpu.VMEM(inverse_low.shape[1:], jnp.bfloat16),
            pltpu.VMEM(inverse_mid.shape[1:], jnp.bfloat16),
            pltpu.VMEM(inverse_top.shape[1:], jnp.bfloat16),
            pltpu.SemaphoreType.DMA((4,)),
            pltpu.SemaphoreType.DMA((slots,)),
            pltpu.SemaphoreType.DMA((slots,)),
            pltpu.SemaphoreType.DMA((slots,)),
            pltpu.SemaphoreType.DMA((slots,)),
        ],
        compiler_params=pltpu.CompilerParams(collective_id=0, has_side_effects=True),
        name="solve",
    )(
        sep_rows[0],
        leaf,
        right_sides[:, 0],
        sep_panels[0],
        inverse_low[0],
        inverse_mid[0],
        inverse_top[0],
    )
    return out[:, None]


def solution(mesh):
    placed = (
        P(("group", "member"), None, None),
        P(("group", "member"), None, None, None, None),
        P(("group", "member"), None, None),
        P(("group", "member"), None, None, None, None),
        P(("group", "member"), None, None),
        P(None, ("group", "member"), None, None),
        P(("group", "member"), None, None),
        P(("group", "member"), None, None),
        P(("group", "member"), None, None),
    )
    return jax.shard_map(
        on_device,
        mesh=mesh,
        in_specs=placed,
        out_specs=P(None, ("group", "member"), None, None),
        check_vma=False,
    )
```

```python
import functools

import jax
import jax.numpy as jnp
from jax import lax
from jax.experimental import pallas as pl
from jax.experimental.pallas import tpu as pltpu
from jax.sharding import PartitionSpec as P

MESH = pl.DeviceIdType.MESH
LEVELS = 3


def solve_kernel(
    members,
    leaf_rows_ref,
    rows_ref,
    values_ref,
    sides_ref,
    leaf_hbm,
    panels_hbm,
    low_hbm,
    mid_hbm,
    top_hbm,
    out_ref,
    base_sums,
    sends,
    parts,
    whole,
    leaf_terms,
    terms,
    leaf_panels,
    panels,
    low,
    mid,
    top,
    local_sem,
    part_send,
    part_recv,
    whole_send,
    whole_recv,
):
    group, member = (lax.axis_index("group"), lax.axis_index("member"))
    blocks, each = (values_ref.shape[0], panels.shape[1])
    inverses = (low, mid, top)
    pairs = [(leaf_hbm.at[:, level], leaf_panels.at[level]) for level in range(LEVELS)]
    pairs += [(low_hbm, low), (panels_hbm, panels), (mid_hbm, mid), (top_hbm, top)]
    loads = [
        pltpu.make_async_copy(source, target, local_sem.at[i])
        for i, (source, target) in enumerate(pairs)
    ]
    for load in loads:
        load.start()

    def place(level):
        count = 2**level
        first_group = group - lax.rem(group, count)
        mine = (group - first_group) * members + member
        return first_group, mine, members * count, members * (count - 1)

    def device(first_group, block):
        return (first_group + lax.div(block, members), lax.rem(block, members))

    def part_copy(level, peer, slot):
        first_group, mine, n, base = place(level)
        return pltpu.make_async_remote_copy(
            src_ref=sends.at[base + peer],
            dst_ref=parts.at[base + slot],
            send_sem=part_send.at[base + peer],
            recv_sem=part_recv.at[base + slot],
            device_id=device(first_group, peer),
            device_id_type=MESH,
        )

    def whole_copy(level, peer, slot):
        first_group, mine, n, base = place(level)
        return pltpu.make_async_remote_copy(
            src_ref=whole.at[base + mine],
            dst_ref=whole.at[base + slot],
            send_sem=whole_send.at[base + peer],
            recv_sem=whole_recv.at[base + slot],
            device_id=device(first_group, peer),
            device_id_type=MESH,
        )

    def leaf_products(level):
        loads[level].wait()

        def one(b, _):
            value = values_ref[b]
            for t in range(each):
                leaf_terms[b * each + t] = jnp.dot(
                    value, leaf_panels[level, b, t], preferred_element_type=jnp.float32
                )
            return 0

        lax.fori_loop(0, blocks, one, 0)

    def leaf_sum(level, q):
        total = jnp.zeros(out_ref.shape[1:], jnp.float32)
        for b in range(blocks):
            for t in range(each):
                hit = (leaf_rows_ref[level, t, b] == q).astype(jnp.float32)
                total = total + leaf_terms[b * each + t] * hit
        return total

    def term_sum(total, slot, j, q):
        for t in range(each):
            hit = (rows_ref[j, 0, t] == q).astype(jnp.float32)
            total = total + terms[slot * each + t] * hit
        return total

    def products(value, slot, j):
        for t in range(each):
            terms[slot * each + t] = jnp.dot(
                value, panels[j, t], preferred_element_type=jnp.float32
            )

    def leaf_base(level):
        _, mine, n, base = place(level)
        leaf_products(level)

        def one(q, _):
            base_sums[base - members + q] = leaf_sum(level, q)
            return 0

        lax.fori_loop(0, n, one, 0)

    def settle(level, partial, first_filler, second_filler):
        _, mine, n, base = place(level)

        def send(k, _):
            peer = lax.rem(mine + k, n)
            sends[base + peer] = partial(peer).astype(jnp.bfloat16)

            @pl.when(k > 1)
            def _():
                part_copy(level, lax.rem(mine + k - 1, n), mine).start()

            return 0

        lax.fori_loop(1, n, send, 0)
        total = partial(mine)
        part_copy(level, lax.rem(mine + n - 1, n), mine).start()
        first_filler()

        def add(k, total):
            peer = lax.rem(mine + n - k, n)
            part_copy(level, peer, peer).wait_recv()
            return total + parts[base + peer].astype(jnp.float32)

        total = lax.fori_loop(1, n, add, total)
        whole[base + mine] = (sides_ref[level].astype(jnp.float32) - total).astype(jnp.bfloat16)

        def tell(k, _):
            whole_copy(level, lax.rem(mine + k, n), mine).start()
            return 0

        lax.fori_loop(1, n, tell, 0)
        second_filler()
        inverse = inverses[level]
        width = inverse.shape[1]

        def multiply(i, total):
            start = i * members

            def hear(c, _):
                @pl.when(start + c != mine)
                def _():
                    whole_copy(level, start + c, start + c).wait_recv()

                return 0

            lax.fori_loop(0, members, hear, 0)
            pieces = [whole[base + start + c] for c in range(members)]
            at = pl.ds(pl.multiple_of(start * width, members * width), members * width)
            return total + jnp.dot(
                jnp.concatenate(pieces, axis=1), inverse[at, :], preferred_element_type=jnp.float32
            )

        total = lax.fori_loop(0, n // members, multiply, jnp.zeros(out_ref.shape[1:], jnp.float32))
        value = total.astype(jnp.bfloat16)
        out_ref[level] = value
        return value

    def drain(level):
        _, mine, n, base = place(level)

        def one(k, _):
            peer = lax.rem(mine + k, n)
            part_copy(level, peer, mine).wait_send()
            whole_copy(level, peer, mine).wait_send()
            return 0

        lax.fori_loop(1, n, one, 0)

    first_group, mine, n, base = place(LEVELS - 1)
    barrier = pltpu.get_barrier_semaphore()

    def greet(k, _):
        pl.semaphore_signal(
            barrier,
            inc=1,
            device_id=device(first_group, lax.rem(mine + k, n)),
            device_id_type=MESH,
        )
        return 0

    lax.fori_loop(1, n, greet, 0)
    leaf_products(0)
    pl.semaphore_wait(barrier, n - 1)

    def rest():
        leaf_base(2)
        for load in loads[LEVELS:]:
            load.wait()

    def early_top():
        products(first, 1, 1)
        _, mine, n, base = place(2)

        def one(q, _):
            base_sums[base - members + q] = term_sum(base_sums[base - members + q], 1, 1, q)
            return 0

        lax.fori_loop(0, n, one, 0)

    def nothing():
        pass

    first = settle(0, lambda q: leaf_sum(0, q), lambda: leaf_base(1), rest)
    products(first, 0, 0)
    second = settle(1, lambda q: term_sum(base_sums[q], 0, 0, q), early_top, nothing)
    products(second, 2, 2)
    settle(2, lambda q: term_sum(base_sums[2 * members + q], 2, 2, q), nothing, nothing)
    for level in range(LEVELS):
        drain(level)


def on_device(
    leaf_solution,
    leaf_panels,
    leaf_rows,
    sep_panels,
    sep_rows,
    right_sides,
    inverse_low,
    inverse_mid,
    inverse_top,
):
    members = lax.axis_size("member")
    blocks, height, width = leaf_solution.shape
    slots = members * (2**LEVELS - 1)
    vmem = pl.BlockSpec(memory_space=pltpu.VMEM)
    smem = pl.BlockSpec(memory_space=pltpu.SMEM)
    hbm = pl.BlockSpec(memory_space=pl.ANY)
    each = sep_panels.shape[2]
    out = pl.pallas_call(
        functools.partial(solve_kernel, members),
        out_shape=jax.ShapeDtypeStruct((LEVELS, height, width), jnp.bfloat16),
        in_specs=[smem, smem, vmem, vmem, hbm, hbm, hbm, hbm, hbm],
        out_specs=vmem,
        scratch_shapes=[
            pltpu.VMEM((slots - members, height, width), jnp.float32),
            pltpu.VMEM((slots, height, width), jnp.bfloat16),
            pltpu.VMEM((slots, height, width), jnp.bfloat16),
            pltpu.VMEM((slots, height, width), jnp.bfloat16),
            pltpu.VMEM((blocks * each, height, width), jnp.float32),
            pltpu.VMEM((LEVELS * each, height, width), jnp.float32),
            pltpu.VMEM((LEVELS, blocks, each, width, width), jnp.bfloat16),
            pltpu.VMEM(sep_panels.shape[1:], jnp.bfloat16),
            pltpu.VMEM(inverse_low.shape[1:], jnp.bfloat16),
            pltpu.VMEM(inverse_mid.shape[1:], jnp.bfloat16),
            pltpu.VMEM(inverse_top.shape[1:], jnp.bfloat16),
            pltpu.SemaphoreType.DMA((LEVELS + 4,)),
            pltpu.SemaphoreType.DMA((slots,)),
            pltpu.SemaphoreType.DMA((slots,)),
            pltpu.SemaphoreType.DMA((slots,)),
            pltpu.SemaphoreType.DMA((slots,)),
        ],
        compiler_params=pltpu.CompilerParams(collective_id=0, has_side_effects=True),
        name="solve",
    )(
        leaf_rows.transpose(1, 2, 0),
        sep_rows.transpose(1, 0, 2),
        leaf_solution,
        right_sides[:, 0],
        leaf_panels,
        sep_panels[0],
        inverse_low[0],
        inverse_mid[0],
        inverse_top[0],
    )
    return out[:, None]


def solution(mesh):
    placed = (
        P(("group", "member"), None, None),
        P(("group", "member"), None, None, None, None),
        P(("group", "member"), None, None),
        P(("group", "member"), None, None, None, None),
        P(("group", "member"), None, None),
        P(None, ("group", "member"), None, None),
        P(("group", "member"), None, None),
        P(("group", "member"), None, None),
        P(("group", "member"), None, None),
    )
    return jax.shard_map(
        on_device,
        mesh=mesh,
        in_specs=placed,
        out_specs=P(None, ("group", "member"), None, None),
        check_vma=False,
    )
```

```python
import functools

import jax
import jax.numpy as jnp
from jax import lax
from jax.experimental import pallas as pl
from jax.experimental.pallas import tpu as pltpu
from jax.sharding import PartitionSpec as P

MESH = pl.DeviceIdType.MESH
LEVELS = 3


def solve_kernel(
    members,
    leaf_rows_ref,
    rows_ref,
    values_ref,
    sides_ref,
    leaf_hbm,
    panels_hbm,
    low_hbm,
    mid_hbm,
    top_hbm,
    out_ref,
    base_sums,
    sends,
    pair,
    parts,
    whole,
    leaf_terms,
    terms,
    leaf_panels,
    panels,
    low,
    mid,
    top,
    local_sem,
    part_send,
    part_recv,
    pair_send,
    pair_recv,
    pass_send,
    whole_send,
    whole_recv,
):
    group, member = (lax.axis_index("group"), lax.axis_index("member"))
    blocks, each = (values_ref.shape[0], panels.shape[1])
    inverses = (low, mid, top)
    pairs = [(leaf_hbm.at[:, level], leaf_panels.at[level]) for level in range(LEVELS)]
    pairs += [(low_hbm, low), (panels_hbm, panels), (mid_hbm, mid), (top_hbm, top)]
    loads = [
        pltpu.make_async_copy(source, target, local_sem.at[i])
        for i, (source, target) in enumerate(pairs)
    ]
    for load in loads:
        load.start()

    def place(level):
        count = 2**level
        step = 2 if level > 0 else 1
        first_group = group - lax.rem(group, count)
        inside = group - first_group
        mine = lax.div(inside, step) * members + member
        size = members * (count // step)
        return first_group, step, lax.rem(inside, step), mine, size, members * (count - 1)

    def group_of(level, index, side):
        return lax.div(index, members) * place(level)[1] + side

    def block(level, index, side):
        return group_of(level, index, side) * members + lax.rem(index, members)

    def device(level, index, side):
        return (place(level)[0] + group_of(level, index, side), lax.rem(index, members))

    def part_copy(level, peer, slot):
        _, _, side, mine, _, base = place(level)
        return pltpu.make_async_remote_copy(
            src_ref=sends.at[base + block(level, peer, side)],
            dst_ref=parts.at[base + slot],
            send_sem=part_send.at[base + peer],
            recv_sem=part_recv.at[base + slot],
            device_id=device(level, peer, side),
            device_id_type=MESH,
        )

    def pair_copy(level, index):
        _, _, side, mine, _, base = place(level)
        return pltpu.make_async_remote_copy(
            src_ref=sends.at[base + block(level, index, 1 - side)],
            dst_ref=pair.at[base + index],
            send_sem=pair_send.at[base + index],
            recv_sem=pair_recv.at[base + index],
            device_id=device(level, mine, 1 - side),
            device_id_type=MESH,
        )

    def whole_copy(level, peer, origin):
        _, _, side, mine, _, base = place(level)
        at = base + block(level, origin, side)
        return pltpu.make_async_remote_copy(
            src_ref=whole.at[at],
            dst_ref=whole.at[at],
            send_sem=whole_send.at[base + peer],
            recv_sem=whole_recv.at[at],
            device_id=device(level, peer, side),
            device_id_type=MESH,
        )

    def pass_copy(level, index, side):
        _, _, own_side, mine, _, base = place(level)
        at = base + block(level, index, side)
        return pltpu.make_async_remote_copy(
            src_ref=whole.at[at],
            dst_ref=whole.at[at],
            send_sem=pass_send.at[base + index],
            recv_sem=whole_recv.at[at],
            device_id=device(level, mine, 1 - own_side),
            device_id_type=MESH,
        )

    def leaf_products(level):
        loads[level].wait()

        def one(b, _):
            value = values_ref[b]
            for t in range(each):
                leaf_terms[b * each + t] = jnp.dot(
                    value, leaf_panels[level, b, t], preferred_element_type=jnp.float32
                )
            return 0

        lax.fori_loop(0, blocks, one, 0)

    def leaf_sum(level, q):
        total = jnp.zeros(out_ref.shape[1:], jnp.float32)
        for b in range(blocks):
            for t in range(each):
                hit = (leaf_rows_ref[level, t, b] == q).astype(jnp.float32)
                total = total + leaf_terms[b * each + t] * hit
        return total

    def term_sum(total, slot, j, q):
        for t in range(each):
            hit = (rows_ref[j, 0, t] == q).astype(jnp.float32)
            total = total + terms[slot * each + t] * hit
        return total

    def products(value, slot, j):
        for t in range(each):
            terms[slot * each + t] = jnp.dot(
                value, panels[j, t], preferred_element_type=jnp.float32
            )

    def leaf_base(level):
        n, base = (members * 2**level, place(level)[-1])
        leaf_products(level)

        def one(q, _):
            base_sums[base - members + q] = leaf_sum(level, q)
            return 0

        lax.fori_loop(0, n, one, 0)

    def settle(level, partial, first_filler, second_filler):
        _, step, side, mine, n, base = place(level)
        paired = step > 1
        if paired:

            def give(k, _):
                at = lax.rem(mine + k, n)
                q = block(level, at, 1 - side)
                sends[base + q] = partial(q).astype(jnp.bfloat16)

                @pl.when(k > 1)
                def _():
                    pair_copy(level, lax.rem(mine + k - 1, n)).start()

                return 0

            lax.fori_loop(1, n + 1, give, 0)
            pair_copy(level, mine).start()

        def joined(at):
            total = partial(block(level, at, side))
            if paired:
                pair_copy(level, at).wait_recv()
                total = total + pair[base + at].astype(jnp.float32)
            return total

        def send(k, _):
            at = lax.rem(mine + k, n)
            sends[base + block(level, at, side)] = joined(at).astype(jnp.bfloat16)

            @pl.when(k > 1)
            def _():
                part_copy(level, lax.rem(mine + k - 1, n), mine).start()

            return 0

        lax.fori_loop(1, n, send, 0)
        part_copy(level, lax.rem(mine + n - 1, n), mine).start()
        total = joined(mine)
        first_filler()

        def add(k, total):
            peer = lax.rem(mine + n - k, n)
            part_copy(level, peer, peer).wait_recv()
            return total + parts[base + peer].astype(jnp.float32)

        total = lax.fori_loop(1, n, add, total)
        whole[base + block(level, mine, side)] = (
            sides_ref[level].astype(jnp.float32) - total
        ).astype(jnp.bfloat16)

        def tell(k, _):
            whole_copy(level, lax.rem(mine + k, n), mine).start()
            return 0

        lax.fori_loop(1, n, tell, 0)
        if paired:
            pass_copy(level, mine, side).start()
        second_filler()

        def hear(k, _):
            peer = lax.rem(mine + n - k, n)
            whole_copy(level, peer, peer).wait_recv()
            if paired:
                pass_copy(level, peer, side).start()
            return 0

        lax.fori_loop(1, n, hear, 0)
        inverse = inverses[level]
        width = inverse.shape[1]

        def multiply(i, total, from_side):
            start = (i * step + from_side) * members
            pieces = [whole[base + start + c] for c in range(members)]
            at = pl.ds(pl.multiple_of(start * width, members * width), members * width)
            return total + jnp.dot(
                jnp.concatenate(pieces, axis=1), inverse[at, :], preferred_element_type=jnp.float32
            )

        total = jnp.zeros(out_ref.shape[1:], jnp.float32)
        total = lax.fori_loop(
            0, n // members, lambda i, total: multiply(i, total, side), total
        )
        if paired:

            def passed(k, _):
                peer = lax.rem(mine + n - k, n)
                pass_copy(level, peer, 1 - side).wait_recv()
                return 0

            lax.fori_loop(0, n, passed, 0)
            total = lax.fori_loop(
                0, n // members, lambda i, total: multiply(i, total, 1 - side), total
            )
        value = total.astype(jnp.bfloat16)
        out_ref[level] = value
        return value

    def drain(level):
        _, step, side, mine, n, base = place(level)

        def one(k, _):
            peer = lax.rem(mine + k, n)
            part_copy(level, peer, mine).wait_send()
            whole_copy(level, peer, mine).wait_send()
            return 0

        lax.fori_loop(1, n, one, 0)
        if step > 1:

            def two(index, _):
                pair_copy(level, index).wait_send()
                pass_copy(level, index, side).wait_send()
                return 0

            lax.fori_loop(0, n, two, 0)

    _, _, side, mine, n, _ = place(LEVELS - 1)
    barrier = pltpu.get_barrier_semaphore()
    pl.semaphore_signal(
        barrier, inc=1, device_id=device(LEVELS - 1, mine, 1 - side), device_id_type=MESH
    )

    def greet(k, _):
        pl.semaphore_signal(
            barrier,
            inc=1,
            device_id=device(LEVELS - 1, lax.rem(mine + k, n), side),
            device_id_type=MESH,
        )
        return 0

    lax.fori_loop(1, n, greet, 0)
    leaf_products(0)
    pl.semaphore_wait(barrier, n)

    def rest():
        leaf_base(2)
        for load in loads[LEVELS:]:
            load.wait()

    def early_top():
        products(first, 1, 1)
        n, base = (members * 4, place(2)[-1])

        def one(q, _):
            base_sums[base - members + q] = term_sum(base_sums[base - members + q], 1, 1, q)
            return 0

        lax.fori_loop(0, n, one, 0)

    def nothing():
        pass

    first = settle(0, lambda q: leaf_sum(0, q), lambda: leaf_base(1), rest)
    products(first, 0, 0)
    second = settle(1, lambda q: term_sum(base_sums[q], 0, 0, q), early_top, nothing)
    products(second, 2, 2)
    settle(2, lambda q: term_sum(base_sums[2 * members + q], 2, 2, q), nothing, nothing)
    for level in range(LEVELS):
        drain(level)


def on_device(
    leaf_solution,
    leaf_panels,
    leaf_rows,
    sep_panels,
    sep_rows,
    right_sides,
    inverse_low,
    inverse_mid,
    inverse_top,
):
    members = lax.axis_size("member")
    blocks, height, width = leaf_solution.shape
    slots = members * (2**LEVELS - 1)
    vmem = pl.BlockSpec(memory_space=pltpu.VMEM)
    smem = pl.BlockSpec(memory_space=pltpu.SMEM)
    hbm = pl.BlockSpec(memory_space=pl.ANY)
    each = sep_panels.shape[2]
    out = pl.pallas_call(
        functools.partial(solve_kernel, members),
        out_shape=jax.ShapeDtypeStruct((LEVELS, height, width), jnp.bfloat16),
        in_specs=[smem, smem, vmem, vmem, hbm, hbm, hbm, hbm, hbm],
        out_specs=vmem,
        scratch_shapes=[
            pltpu.VMEM((slots - members, height, width), jnp.float32),
            pltpu.VMEM((slots, height, width), jnp.bfloat16),
            pltpu.VMEM((slots, height, width), jnp.bfloat16),
            pltpu.VMEM((slots, height, width), jnp.bfloat16),
            pltpu.VMEM((slots, height, width), jnp.bfloat16),
            pltpu.VMEM((blocks * each, height, width), jnp.float32),
            pltpu.VMEM((LEVELS * each, height, width), jnp.float32),
            pltpu.VMEM((LEVELS, blocks, each, width, width), jnp.bfloat16),
            pltpu.VMEM(sep_panels.shape[1:], jnp.bfloat16),
            pltpu.VMEM(inverse_low.shape[1:], jnp.bfloat16),
            pltpu.VMEM(inverse_mid.shape[1:], jnp.bfloat16),
            pltpu.VMEM(inverse_top.shape[1:], jnp.bfloat16),
            pltpu.SemaphoreType.DMA((LEVELS + 4,)),
            pltpu.SemaphoreType.DMA((slots,)),
            pltpu.SemaphoreType.DMA((slots,)),
            pltpu.SemaphoreType.DMA((slots,)),
            pltpu.SemaphoreType.DMA((slots,)),
            pltpu.SemaphoreType.DMA((slots,)),
            pltpu.SemaphoreType.DMA((slots,)),
            pltpu.SemaphoreType.DMA((slots,)),
        ],
        compiler_params=pltpu.CompilerParams(collective_id=0, has_side_effects=True),
        name="solve",
    )(
        leaf_rows.transpose(1, 2, 0),
        sep_rows.transpose(1, 0, 2),
        leaf_solution,
        right_sides[:, 0],
        leaf_panels,
        sep_panels[0],
        inverse_low[0],
        inverse_mid[0],
        inverse_top[0],
    )
    return out[:, None]


def solution(mesh):
    placed = (
        P(("group", "member"), None, None),
        P(("group", "member"), None, None, None, None),
        P(("group", "member"), None, None),
        P(("group", "member"), None, None, None, None),
        P(("group", "member"), None, None),
        P(None, ("group", "member"), None, None),
        P(("group", "member"), None, None),
        P(("group", "member"), None, None),
        P(("group", "member"), None, None),
    )
    return jax.shard_map(
        on_device,
        mesh=mesh,
        in_specs=placed,
        out_specs=P(None, ("group", "member"), None, None),
        check_vma=False,
    )
```

```python
import functools

import jax
import jax.numpy as jnp
from jax import lax
from jax.experimental import pallas as pl
from jax.experimental.pallas import tpu as pltpu
from jax.sharding import PartitionSpec as P

MESH = pl.DeviceIdType.MESH
LEVELS = 3


def solve_kernel(
    members,
    leaf_rows_ref,
    rows_ref,
    values_ref,
    sides_ref,
    leaf_hbm,
    panels_hbm,
    low_hbm,
    mid_hbm,
    top_hbm,
    out_ref,
    base_sums,
    sends,
    pair,
    parts,
    whole,
    leaf_terms,
    terms,
    leaf_panels,
    panels,
    low,
    mid,
    top,
    local_sem,
    part_send,
    part_recv,
    pair_send,
    pair_recv,
    pass_send,
    whole_send,
    whole_recv,
):
    group, member = (lax.axis_index("group"), lax.axis_index("member"))
    blocks, each = (values_ref.shape[0], panels.shape[1])
    inverses = (low, mid, top)
    pairs = [(leaf_hbm.at[:, level], leaf_panels.at[level]) for level in range(LEVELS)]
    pairs += [(low_hbm, low), (panels_hbm, panels), (mid_hbm, mid), (top_hbm, top)]
    loads = [
        pltpu.make_async_copy(source, target, local_sem.at[i])
        for i, (source, target) in enumerate(pairs)
    ]
    loads[0].start()

    def place(level):
        count = 2**level
        step = 2 if level > 0 else 1
        first_group = group - lax.rem(group, count)
        inside = group - first_group
        mine = lax.div(inside, step) * members + member
        size = members * (count // step)
        return first_group, step, lax.rem(inside, step), mine, size, members * (count - 1)

    def group_of(level, index, side):
        return lax.div(index, members) * place(level)[1] + side

    def block(level, index, side):
        return group_of(level, index, side) * members + lax.rem(index, members)

    def device(level, index, side):
        return (place(level)[0] + group_of(level, index, side), lax.rem(index, members))

    def part_copy(level, peer, slot):
        _, _, side, mine, _, base = place(level)
        return pltpu.make_async_remote_copy(
            src_ref=sends.at[base + block(level, peer, side)],
            dst_ref=parts.at[base + slot],
            send_sem=part_send.at[base + peer],
            recv_sem=part_recv.at[base + slot],
            device_id=device(level, peer, side),
            device_id_type=MESH,
        )

    def pair_copy(level, index):
        _, _, side, mine, _, base = place(level)
        return pltpu.make_async_remote_copy(
            src_ref=sends.at[base + block(level, index, 1 - side)],
            dst_ref=pair.at[base + index],
            send_sem=pair_send.at[base + index],
            recv_sem=pair_recv.at[base + index],
            device_id=device(level, mine, 1 - side),
            device_id_type=MESH,
        )

    def whole_copy(level, peer, origin):
        _, _, side, mine, _, base = place(level)
        at = base + block(level, origin, side)
        return pltpu.make_async_remote_copy(
            src_ref=whole.at[at],
            dst_ref=whole.at[at],
            send_sem=whole_send.at[base + peer],
            recv_sem=whole_recv.at[at],
            device_id=device(level, peer, side),
            device_id_type=MESH,
        )

    def pass_copy(level, index, side):
        _, _, own_side, mine, _, base = place(level)
        at = base + block(level, index, side)
        return pltpu.make_async_remote_copy(
            src_ref=whole.at[at],
            dst_ref=whole.at[at],
            send_sem=pass_send.at[base + index],
            recv_sem=whole_recv.at[at],
            device_id=device(level, mine, 1 - own_side),
            device_id_type=MESH,
        )

    def leaf_products(level):
        height, width = out_ref.shape[1:]
        for b in range(blocks):
            joined = jnp.concatenate([leaf_panels[level, b, t] for t in range(each)], axis=1)
            product = jnp.dot(values_ref[b], joined, preferred_element_type=jnp.float32)
            for t in range(each):
                leaf_terms[b * each + t] = product[:, t * width : (t + 1) * width]

    def leaf_sum(level, q):
        total = jnp.zeros(out_ref.shape[1:], jnp.float32)
        for b in range(blocks):
            for t in range(each):
                hit = (leaf_rows_ref[level, t, b] == q).astype(jnp.float32)
                total = total + leaf_terms[b * each + t] * hit
        return total

    def term_sum(total, slot, j, q):
        for t in range(each):
            hit = (rows_ref[j, 0, t] == q).astype(jnp.float32)
            total = total + terms[slot * each + t] * hit
        return total

    def products(value, slot, j):
        for t in range(each):
            terms[slot * each + t] = jnp.dot(
                value, panels[j, t], preferred_element_type=jnp.float32
            )

    def leaf_base(level, more):
        n, base = (members * 2**level, place(level)[-1])

        def one(q, _):
            base_sums[base - members + q] = more(leaf_sum(level, q), q)
            return 0

        lax.fori_loop(0, n, one, 0)

    def settle(level, partial, first_filler, second_filler):
        _, step, side, mine, n, base = place(level)
        paired = step > 1
        if paired:

            def give(k, _):
                at = lax.rem(mine + k, n)
                q = block(level, at, 1 - side)
                sends[base + q] = partial(q).astype(jnp.bfloat16)

                @pl.when(k > 1)
                def _():
                    pair_copy(level, lax.rem(mine + k - 1, n)).start()

                return 0

            lax.fori_loop(1, n + 1, give, 0)
            pair_copy(level, mine).start()

        def joined(at):
            total = partial(block(level, at, side))
            if paired:
                pair_copy(level, at).wait_recv()
                total = total + pair[base + at].astype(jnp.float32)
            return total

        def send(k, _):
            at = lax.rem(mine + k, n)
            if paired:
                sends[base + block(level, at, side)] = joined(at).astype(jnp.bfloat16)

            @pl.when(k > 1)
            def _():
                part_copy(level, lax.rem(mine + k - 1, n), mine).start()

            return 0

        lax.fori_loop(1, n, send, 0)
        part_copy(level, lax.rem(mine + n - 1, n), mine).start()
        total = joined(mine)
        first_filler()

        def add(k, total):
            peer = lax.rem(mine + n - k, n)
            part_copy(level, peer, peer).wait_recv()
            return total + parts[base + peer].astype(jnp.float32)

        total = lax.fori_loop(1, n, add, total)
        whole[base + block(level, mine, side)] = (
            sides_ref[level].astype(jnp.float32) - total
        ).astype(jnp.bfloat16)

        def tell(k, _):
            whole_copy(level, lax.rem(mine + k, n), mine).start()
            return 0

        lax.fori_loop(1, n, tell, 0)
        if paired:
            pass_copy(level, mine, side).start()
        second_filler()

        def hear(k, _):
            peer = lax.rem(mine + n - k, n)
            whole_copy(level, peer, peer).wait_recv()
            if paired:
                pass_copy(level, peer, side).start()
            return 0

        lax.fori_loop(1, n, hear, 0)
        inverse = inverses[level]
        width = inverse.shape[1]

        def multiply(i, total, from_side):
            start = (i * step + from_side) * members
            pieces = [whole[base + start + c] for c in range(members)]
            at = pl.ds(pl.multiple_of(start * width, members * width), members * width)
            return total + jnp.dot(
                jnp.concatenate(pieces, axis=1), inverse[at, :], preferred_element_type=jnp.float32
            )

        total = jnp.zeros(out_ref.shape[1:], jnp.float32)
        total = lax.fori_loop(
            0, n // members, lambda i, total: multiply(i, total, side), total
        )
        if paired:

            def passed(k, _):
                peer = lax.rem(mine + n - k, n)
                pass_copy(level, peer, 1 - side).wait_recv()
                return 0

            lax.fori_loop(0, n, passed, 0)
            total = lax.fori_loop(
                0, n // members, lambda i, total: multiply(i, total, 1 - side), total
            )
        value = total.astype(jnp.bfloat16)
        out_ref[level] = value
        return value

    def drain(level):
        _, step, side, mine, n, base = place(level)

        def one(k, _):
            peer = lax.rem(mine + k, n)
            part_copy(level, peer, mine).wait_send()
            whole_copy(level, peer, mine).wait_send()
            return 0

        lax.fori_loop(1, n, one, 0)
        if step > 1:

            def two(index, _):
                pair_copy(level, index).wait_send()
                pass_copy(level, index, side).wait_send()
                return 0

            lax.fori_loop(0, n, two, 0)

    _, _, side, mine, n, _ = place(LEVELS - 1)
    barrier = pltpu.get_barrier_semaphore()
    pl.semaphore_signal(
        barrier, inc=1, device_id=device(LEVELS - 1, mine, 1 - side), device_id_type=MESH
    )

    def greet(k, _):
        pl.semaphore_signal(
            barrier,
            inc=1,
            device_id=device(LEVELS - 1, lax.rem(mine + k, n), side),
            device_id_type=MESH,
        )
        return 0

    lax.fori_loop(1, n, greet, 0)
    loads[0].wait()
    for load in loads[1:]:
        load.start()
    leaf_products(0)

    def ready(q, _):
        sends[q] = leaf_sum(0, q).astype(jnp.bfloat16)
        return 0

    lax.fori_loop(0, members, ready, 0)
    pl.semaphore_wait(barrier, n)

    def base_mid():
        loads[1].wait()
        leaf_products(1)
        leaf_base(1, lambda total, q: total)

    def products_top():
        for load in loads[2:]:
            load.wait()
        leaf_products(2)

    def base_top():
        products(first, 1, 1)
        leaf_base(2, lambda total, q: term_sum(total, 1, 1, q))

    def nothing():
        pass

    first = settle(0, lambda q: leaf_sum(0, q), base_mid, products_top)
    products(first, 0, 0)
    second = settle(1, lambda q: term_sum(base_sums[q], 0, 0, q), base_top, nothing)
    products(second, 2, 2)
    settle(2, lambda q: term_sum(base_sums[2 * members + q], 2, 2, q), nothing, nothing)
    for level in range(LEVELS):
        drain(level)


def on_device(
    leaf_solution,
    leaf_panels,
    leaf_rows,
    sep_panels,
    sep_rows,
    right_sides,
    inverse_low,
    inverse_mid,
    inverse_top,
):
    members = lax.axis_size("member")
    blocks, height, width = leaf_solution.shape
    slots = members * (2**LEVELS - 1)
    vmem = pl.BlockSpec(memory_space=pltpu.VMEM)
    smem = pl.BlockSpec(memory_space=pltpu.SMEM)
    hbm = pl.BlockSpec(memory_space=pl.ANY)
    each = sep_panels.shape[2]
    out = pl.pallas_call(
        functools.partial(solve_kernel, members),
        out_shape=jax.ShapeDtypeStruct((LEVELS, height, width), jnp.bfloat16),
        in_specs=[smem, smem, vmem, vmem, hbm, hbm, hbm, hbm, hbm],
        out_specs=vmem,
        scratch_shapes=[
            pltpu.VMEM((slots - members, height, width), jnp.float32),
            pltpu.VMEM((slots, height, width), jnp.bfloat16),
            pltpu.VMEM((slots, height, width), jnp.bfloat16),
            pltpu.VMEM((slots, height, width), jnp.bfloat16),
            pltpu.VMEM((slots, height, width), jnp.bfloat16),
            pltpu.VMEM((blocks * each, height, width), jnp.float32),
            pltpu.VMEM((LEVELS * each, height, width), jnp.float32),
            pltpu.VMEM((LEVELS, blocks, each, width, width), jnp.bfloat16),
            pltpu.VMEM(sep_panels.shape[1:], jnp.bfloat16),
            pltpu.VMEM(inverse_low.shape[1:], jnp.bfloat16),
            pltpu.VMEM(inverse_mid.shape[1:], jnp.bfloat16),
            pltpu.VMEM(inverse_top.shape[1:], jnp.bfloat16),
            pltpu.SemaphoreType.DMA((LEVELS + 4,)),
            pltpu.SemaphoreType.DMA((slots,)),
            pltpu.SemaphoreType.DMA((slots,)),
            pltpu.SemaphoreType.DMA((slots,)),
            pltpu.SemaphoreType.DMA((slots,)),
            pltpu.SemaphoreType.DMA((slots,)),
            pltpu.SemaphoreType.DMA((slots,)),
            pltpu.SemaphoreType.DMA((slots,)),
        ],
        compiler_params=pltpu.CompilerParams(collective_id=0, has_side_effects=True),
        name="solve",
    )(
        leaf_rows.transpose(1, 2, 0),
        sep_rows.transpose(1, 0, 2),
        leaf_solution,
        right_sides[:, 0],
        leaf_panels,
        sep_panels[0],
        inverse_low[0],
        inverse_mid[0],
        inverse_top[0],
    )
    return out[:, None]


def solution(mesh):
    placed = (
        P(("group", "member"), None, None),
        P(("group", "member"), None, None, None, None),
        P(("group", "member"), None, None),
        P(("group", "member"), None, None, None, None),
        P(("group", "member"), None, None),
        P(None, ("group", "member"), None, None),
        P(("group", "member"), None, None),
        P(("group", "member"), None, None),
        P(("group", "member"), None, None),
    )
    return jax.shard_map(
        on_device,
        mesh=mesh,
        in_specs=placed,
        out_specs=P(None, ("group", "member"), None, None),
        check_vma=False,
    )
```

```python
import functools

import jax
import jax.numpy as jnp
from jax import lax
from jax.experimental import pallas as pl
from jax.experimental.pallas import tpu as pltpu
from jax.sharding import PartitionSpec as P

MESH = pl.DeviceIdType.MESH
LEVELS = 3


def solve_kernel(
    members,
    leaf_rows_ref,
    rows_ref,
    values_ref,
    sides_ref,
    leaf_hbm,
    panels_hbm,
    low_hbm,
    mid_hbm,
    top_hbm,
    out_ref,
    base_sums,
    sends,
    pair,
    parts,
    whole,
    leaf_terms,
    terms,
    leaf_panels,
    panels,
    low,
    mid,
    top,
    local_sem,
    part_send,
    part_recv,
    pair_send,
    pair_recv,
    pass_send,
    whole_send,
    whole_recv,
):
    group, member = (lax.axis_index("group"), lax.axis_index("member"))
    blocks, each = (values_ref.shape[0], panels.shape[1])
    inverses = (low, mid, top)
    pairs = [(leaf_hbm.at[:, level], leaf_panels.at[level]) for level in range(LEVELS)]
    pairs += [(low_hbm, low), (panels_hbm, panels), (mid_hbm, mid), (top_hbm, top)]
    loads = [
        pltpu.make_async_copy(source, target, local_sem.at[i])
        for i, (source, target) in enumerate(pairs)
    ]
    loads[0].start()

    def place(level):
        count = 2**level
        step = 2 if level > 0 else 1
        first_group = group - lax.rem(group, count)
        inside = group - first_group
        mine = lax.div(inside, step) * members + member
        size = members * (count // step)
        return first_group, step, lax.rem(inside, step), mine, size, members * (count - 1)

    def group_of(level, index, side):
        return lax.div(index, members) * place(level)[1] + side

    def block(level, index, side):
        return group_of(level, index, side) * members + lax.rem(index, members)

    def device(level, index, side):
        return (place(level)[0] + group_of(level, index, side), lax.rem(index, members))

    def exchange(level, k, hearing=False):
        _, _, _, mine, n, _ = place(level)
        if n & (n - 1):
            return lax.rem(mine + (n - k if hearing else k), n)
        rows = n // members
        left = n - k
        mask = lax.rem(left, rows) * members + lax.div(left, rows)
        peer = 0
        bit = 1
        while bit < n:
            peer = peer + bit * lax.rem(lax.div(mine, bit) + lax.div(mask, bit), 2)
            bit *= 2
        return peer

    def part_copy(level, peer, slot):
        _, _, side, mine, _, base = place(level)
        return pltpu.make_async_remote_copy(
            src_ref=sends.at[base + block(level, peer, side)],
            dst_ref=parts.at[base + slot],
            send_sem=part_send.at[base + peer],
            recv_sem=part_recv.at[base + slot],
            device_id=device(level, peer, side),
            device_id_type=MESH,
        )

    def pair_copy(level, index):
        _, _, side, mine, _, base = place(level)
        return pltpu.make_async_remote_copy(
            src_ref=sends.at[base + block(level, index, 1 - side)],
            dst_ref=pair.at[base + index],
            send_sem=pair_send.at[base + index],
            recv_sem=pair_recv.at[base + index],
            device_id=device(level, mine, 1 - side),
            device_id_type=MESH,
        )

    def whole_copy(level, peer, origin):
        _, _, side, mine, _, base = place(level)
        at = base + block(level, origin, side)
        return pltpu.make_async_remote_copy(
            src_ref=whole.at[at],
            dst_ref=whole.at[at],
            send_sem=whole_send.at[base + peer],
            recv_sem=whole_recv.at[at],
            device_id=device(level, peer, side),
            device_id_type=MESH,
        )

    def pass_copy(level, index, side):
        _, _, own_side, mine, _, base = place(level)
        at = base + block(level, index, side)
        return pltpu.make_async_remote_copy(
            src_ref=whole.at[at],
            dst_ref=whole.at[at],
            send_sem=pass_send.at[base + index],
            recv_sem=whole_recv.at[at],
            device_id=device(level, mine, 1 - own_side),
            device_id_type=MESH,
        )

    def leaf_products(level):
        height, width = out_ref.shape[1:]
        for b in range(blocks):
            joined = jnp.concatenate([leaf_panels[level, b, t] for t in range(each)], axis=1)
            product = jnp.dot(values_ref[b], joined, preferred_element_type=jnp.float32)
            for t in range(each):
                leaf_terms[b * each + t] = product[:, t * width : (t + 1) * width]

    def leaf_sum(level, q):
        total = jnp.zeros(out_ref.shape[1:], jnp.float32)
        for b in range(blocks):
            for t in range(each):
                hit = (leaf_rows_ref[level, t, b] == q).astype(jnp.float32)
                total = total + leaf_terms[b * each + t] * hit
        return total

    def term_sum(total, slot, j, q):
        for t in range(each):
            hit = (rows_ref[j, 0, t] == q).astype(jnp.float32)
            total = total + terms[slot * each + t] * hit
        return total

    def products(value, slot, j):
        for t in range(each):
            terms[slot * each + t] = jnp.dot(
                value, panels[j, t], preferred_element_type=jnp.float32
            )

    def leaf_base(level, more):
        n, base = (members * 2**level, place(level)[-1])

        def one(q, _):
            base_sums[base - members + q] = more(leaf_sum(level, q), q)
            return 0

        lax.fori_loop(0, n, one, 0)

    def settle(level, partial, first_filler, second_filler):
        _, step, side, mine, n, base = place(level)
        paired = step > 1
        if paired:

            def give(k, _):
                at = exchange(level, k)
                q = block(level, at, 1 - side)
                sends[base + q] = partial(q).astype(jnp.bfloat16)

                @pl.when(k > 1)
                def _():
                    pair_copy(level, exchange(level, k - 1)).start()

                return 0

            lax.fori_loop(1, n + 1, give, 0)
            pair_copy(level, mine).start()

        def joined(at):
            total = partial(block(level, at, side))
            if paired:
                pair_copy(level, at).wait_recv()
                total = total + pair[base + at].astype(jnp.float32)
            return total

        def send(k, _):
            at = exchange(level, k)
            if paired:
                sends[base + block(level, at, side)] = joined(at).astype(jnp.bfloat16)

            @pl.when(k > 1)
            def _():
                part_copy(level, exchange(level, k - 1), mine).start()

            return 0

        lax.fori_loop(1, n, send, 0)
        part_copy(level, exchange(level, n - 1), mine).start()
        total = joined(mine)
        first_filler()

        def add(k, total):
            peer = exchange(level, k, True)
            part_copy(level, peer, peer).wait_recv()
            return total + parts[base + peer].astype(jnp.float32)

        total = lax.fori_loop(1, n, add, total)
        whole[base + block(level, mine, side)] = (
            sides_ref[level].astype(jnp.float32) - total
        ).astype(jnp.bfloat16)

        def tell(k, _):
            whole_copy(level, exchange(level, k), mine).start()
            return 0

        lax.fori_loop(1, n, tell, 0)
        if paired:
            pass_copy(level, mine, side).start()
        second_filler()

        def hear(k, _):
            peer = exchange(level, k, True)
            whole_copy(level, peer, peer).wait_recv()
            if paired:
                pass_copy(level, peer, side).start()
            return 0

        lax.fori_loop(1, n, hear, 0)
        inverse = inverses[level]
        width = inverse.shape[1]

        def multiply(i, total, from_side):
            start = (i * step + from_side) * members
            pieces = [whole[base + start + c] for c in range(members)]
            at = pl.ds(pl.multiple_of(start * width, members * width), members * width)
            return total + jnp.dot(
                jnp.concatenate(pieces, axis=1), inverse[at, :], preferred_element_type=jnp.float32
            )

        total = jnp.zeros(out_ref.shape[1:], jnp.float32)
        total = lax.fori_loop(
            0, n // members, lambda i, total: multiply(i, total, side), total
        )
        if paired:

            def passed(k, _):
                pass_copy(level, k, 1 - side).wait_recv()
                return 0

            lax.fori_loop(0, n, passed, 0)
            total = lax.fori_loop(
                0, n // members, lambda i, total: multiply(i, total, 1 - side), total
            )
        value = total.astype(jnp.bfloat16)
        out_ref[level] = value
        return value

    def drain(level):
        _, step, side, mine, n, base = place(level)

        def one(k, _):
            peer = exchange(level, k)
            part_copy(level, peer, mine).wait_send()
            whole_copy(level, peer, mine).wait_send()
            return 0

        lax.fori_loop(1, n, one, 0)
        if step > 1:

            def two(index, _):
                pair_copy(level, index).wait_send()
                pass_copy(level, index, side).wait_send()
                return 0

            lax.fori_loop(0, n, two, 0)

    _, _, side, mine, n, _ = place(LEVELS - 1)
    barrier = pltpu.get_barrier_semaphore()
    pl.semaphore_signal(
        barrier, inc=1, device_id=device(LEVELS - 1, mine, 1 - side), device_id_type=MESH
    )

    def greet(k, _):
        pl.semaphore_signal(
            barrier,
            inc=1,
            device_id=device(LEVELS - 1, exchange(LEVELS - 1, k), side),
            device_id_type=MESH,
        )
        return 0

    lax.fori_loop(1, n, greet, 0)
    loads[0].wait()
    for load in loads[1:]:
        load.start()
    leaf_products(0)

    def ready(q, _):
        sends[q] = leaf_sum(0, q).astype(jnp.bfloat16)
        return 0

    lax.fori_loop(0, members, ready, 0)
    pl.semaphore_wait(barrier, n)

    def base_mid():
        loads[1].wait()
        leaf_products(1)
        leaf_base(1, lambda total, q: total)

    def products_top():
        for load in loads[2:]:
            load.wait()
        leaf_products(2)

    def base_top():
        products(first, 1, 1)
        leaf_base(2, lambda total, q: term_sum(total, 1, 1, q))

    def nothing():
        pass

    first = settle(0, lambda q: leaf_sum(0, q), base_mid, products_top)
    products(first, 0, 0)
    second = settle(1, lambda q: term_sum(base_sums[q], 0, 0, q), base_top, nothing)
    products(second, 2, 2)
    settle(2, lambda q: term_sum(base_sums[2 * members + q], 2, 2, q), nothing, nothing)
    for level in range(LEVELS):
        drain(level)


def on_device(
    leaf_solution,
    leaf_panels,
    leaf_rows,
    sep_panels,
    sep_rows,
    right_sides,
    inverse_low,
    inverse_mid,
    inverse_top,
):
    members = lax.axis_size("member")
    blocks, height, width = leaf_solution.shape
    slots = members * (2**LEVELS - 1)
    vmem = pl.BlockSpec(memory_space=pltpu.VMEM)
    smem = pl.BlockSpec(memory_space=pltpu.SMEM)
    hbm = pl.BlockSpec(memory_space=pl.ANY)
    each = sep_panels.shape[2]
    out = pl.pallas_call(
        functools.partial(solve_kernel, members),
        out_shape=jax.ShapeDtypeStruct((LEVELS, height, width), jnp.bfloat16),
        in_specs=[smem, smem, vmem, vmem, hbm, hbm, hbm, hbm, hbm],
        out_specs=vmem,
        scratch_shapes=[
            pltpu.VMEM((slots - members, height, width), jnp.float32),
            pltpu.VMEM((slots, height, width), jnp.bfloat16),
            pltpu.VMEM((slots, height, width), jnp.bfloat16),
            pltpu.VMEM((slots, height, width), jnp.bfloat16),
            pltpu.VMEM((slots, height, width), jnp.bfloat16),
            pltpu.VMEM((blocks * each, height, width), jnp.float32),
            pltpu.VMEM((LEVELS * each, height, width), jnp.float32),
            pltpu.VMEM((LEVELS, blocks, each, width, width), jnp.bfloat16),
            pltpu.VMEM(sep_panels.shape[1:], jnp.bfloat16),
            pltpu.VMEM(inverse_low.shape[1:], jnp.bfloat16),
            pltpu.VMEM(inverse_mid.shape[1:], jnp.bfloat16),
            pltpu.VMEM(inverse_top.shape[1:], jnp.bfloat16),
            pltpu.SemaphoreType.DMA((LEVELS + 4,)),
            pltpu.SemaphoreType.DMA((slots,)),
            pltpu.SemaphoreType.DMA((slots,)),
            pltpu.SemaphoreType.DMA((slots,)),
            pltpu.SemaphoreType.DMA((slots,)),
            pltpu.SemaphoreType.DMA((slots,)),
            pltpu.SemaphoreType.DMA((slots,)),
            pltpu.SemaphoreType.DMA((slots,)),
        ],
        compiler_params=pltpu.CompilerParams(collective_id=0, has_side_effects=True),
        name="solve",
    )(
        leaf_rows.transpose(1, 2, 0),
        sep_rows.transpose(1, 0, 2),
        leaf_solution,
        right_sides[:, 0],
        leaf_panels,
        sep_panels[0],
        inverse_low[0],
        inverse_mid[0],
        inverse_top[0],
    )
    return out[:, None]


def solution(mesh):
    placed = (
        P(("group", "member"), None, None),
        P(("group", "member"), None, None, None, None),
        P(("group", "member"), None, None),
        P(("group", "member"), None, None, None, None),
        P(("group", "member"), None, None),
        P(None, ("group", "member"), None, None),
        P(("group", "member"), None, None),
        P(("group", "member"), None, None),
        P(("group", "member"), None, None),
    )
    return jax.shard_map(
        on_device,
        mesh=mesh,
        in_specs=placed,
        out_specs=P(None, ("group", "member"), None, None),
        check_vma=False,
    )
```

```python
import functools

import jax
import jax.numpy as jnp
from jax import lax
from jax.experimental import pallas as pl
from jax.experimental.pallas import tpu as pltpu
from jax.sharding import PartitionSpec as P

MESH = pl.DeviceIdType.MESH
LEVELS = 3


def solve_kernel(
    members,
    leaf_rows_ref,
    rows_ref,
    values_ref,
    sides_ref,
    leaf_hbm,
    panels_hbm,
    low_hbm,
    mid_hbm,
    top_hbm,
    out_ref,
    base_sums,
    sends,
    pair,
    parts,
    whole,
    leaf_terms,
    terms,
    leaf_panels,
    panels,
    low,
    mid,
    top,
    local_sem,
    part_send,
    part_recv,
    pair_send,
    pair_recv,
    pass_send,
    whole_send,
    whole_recv,
):
    group, member = (lax.axis_index("group"), lax.axis_index("member"))
    blocks, each = (values_ref.shape[0], panels.shape[1])
    inverses = (low, mid, top)
    pairs = [(leaf_hbm.at[:, level], leaf_panels.at[level]) for level in range(LEVELS)]
    pairs += [(low_hbm, low), (panels_hbm, panels), (mid_hbm, mid), (top_hbm, top)]
    loads = [
        pltpu.make_async_copy(source, target, local_sem.at[i])
        for i, (source, target) in enumerate(pairs)
    ]
    loads[0].start()

    def place(level):
        count = 2**level
        step = 2 if level > 0 else 1
        first_group = group - lax.rem(group, count)
        inside = group - first_group
        mine = lax.div(inside, step) * members + member
        size = members * (count // step)
        return first_group, step, lax.rem(inside, step), mine, size, members * (count - 1)

    def group_of(level, index, side):
        return lax.div(index, members) * place(level)[1] + side

    def block(level, index, side):
        return group_of(level, index, side) * members + lax.rem(index, members)

    def device(level, index, side):
        return (place(level)[0] + group_of(level, index, side), lax.rem(index, members))

    def exchange(level, k, hearing=False):
        _, _, _, mine, n, _ = place(level)
        if n & (n - 1):
            return lax.rem(mine + (n - k if hearing else k), n)
        rows = n // members
        left = n - k
        mask = lax.rem(left, rows) * members + lax.div(left, rows)
        peer = 0
        bit = 1
        while bit < n:
            peer = peer + bit * lax.rem(lax.div(mine, bit) + lax.div(mask, bit), 2)
            bit *= 2
        return peer

    def part_copy(level, peer, slot):
        _, _, side, mine, _, base = place(level)
        return pltpu.make_async_remote_copy(
            src_ref=sends.at[base + block(level, peer, side)],
            dst_ref=parts.at[base + slot],
            send_sem=part_send.at[base + peer],
            recv_sem=part_recv.at[base + slot],
            device_id=device(level, peer, side),
            device_id_type=MESH,
        )

    def pair_copy(level, index):
        _, _, side, mine, _, base = place(level)
        return pltpu.make_async_remote_copy(
            src_ref=sends.at[base + block(level, index, 1 - side)],
            dst_ref=pair.at[base + index],
            send_sem=pair_send.at[base + index],
            recv_sem=pair_recv.at[base + index],
            device_id=device(level, mine, 1 - side),
            device_id_type=MESH,
        )

    def whole_copy(level, peer, origin):
        _, _, side, mine, _, base = place(level)
        at = base + block(level, origin, side)
        return pltpu.make_async_remote_copy(
            src_ref=whole.at[at],
            dst_ref=whole.at[at],
            send_sem=whole_send.at[base + peer],
            recv_sem=whole_recv.at[at],
            device_id=device(level, peer, side),
            device_id_type=MESH,
        )

    def pass_copy(level, index, side):
        _, _, own_side, mine, _, base = place(level)
        at = base + block(level, index, side)
        return pltpu.make_async_remote_copy(
            src_ref=whole.at[at],
            dst_ref=whole.at[at],
            send_sem=pass_send.at[base + index],
            recv_sem=whole_recv.at[at],
            device_id=device(level, mine, 1 - own_side),
            device_id_type=MESH,
        )

    def leaf_products(level):
        height, width = out_ref.shape[1:]
        for b in range(blocks):
            joined = jnp.concatenate([leaf_panels[level, b, t] for t in range(each)], axis=1)
            product = jnp.dot(values_ref[b], joined, preferred_element_type=jnp.float32)
            for t in range(each):
                leaf_terms[b * each + t] = product[:, t * width : (t + 1) * width]

    def leaf_sum(level, q):
        total = jnp.zeros(out_ref.shape[1:], jnp.float32)
        for b in range(blocks):
            for t in range(each):
                hit = (leaf_rows_ref[level, t, b] == q).astype(jnp.float32)
                total = total + leaf_terms[b * each + t] * hit
        return total

    def term_sum(total, slot, j, q):
        for t in range(each):
            hit = (rows_ref[j, 0, t] == q).astype(jnp.float32)
            total = total + terms[slot * each + t] * hit
        return total

    def products(value, slot, j):
        for t in range(each):
            terms[slot * each + t] = jnp.dot(
                value, panels[j, t], preferred_element_type=jnp.float32
            )

    def leaf_base(level, more):
        n, base = (members * 2**level, place(level)[-1])

        def one(q, _):
            base_sums[base - members + q] = more(leaf_sum(level, q), q)
            return 0

        lax.fori_loop(0, n, one, 0)

    def settle(level, partial, first_filler, second_filler):
        _, step, side, mine, n, base = place(level)
        paired = step > 1
        if paired:

            def give(k, _):
                at = exchange(level, k)
                q = block(level, at, 1 - side)
                sends[base + q] = partial(q).astype(jnp.bfloat16)

                @pl.when(k > 1)
                def _():
                    pair_copy(level, exchange(level, k - 1)).start()

                return 0

            lax.fori_loop(1, n + 1, give, 0)
            pair_copy(level, mine).start()

        def joined(at):
            total = partial(block(level, at, side))
            if paired:
                pair_copy(level, at).wait_recv()
                total = total + pair[base + at].astype(jnp.float32)
            return total

        def send(k, _):
            at = exchange(level, k)
            if paired:
                sends[base + block(level, at, side)] = joined(at).astype(jnp.bfloat16)

            @pl.when(k > 1)
            def _():
                part_copy(level, exchange(level, k - 1), mine).start()

            return 0

        lax.fori_loop(1, n, send, 0)
        part_copy(level, exchange(level, n - 1), mine).start()
        total = joined(mine)
        first_filler()

        def add(k, total):
            peer = exchange(level, k, True)
            part_copy(level, peer, peer).wait_recv()
            return total + parts[base + peer].astype(jnp.float32)

        total = lax.fori_loop(1, n, add, total, unroll=n <= 2 * members)
        whole[base + block(level, mine, side)] = (
            sides_ref[level].astype(jnp.float32) - total
        ).astype(jnp.bfloat16)

        def tell(k, _):
            whole_copy(level, exchange(level, k), mine).start()
            return 0

        lax.fori_loop(1, n, tell, 0, unroll=n <= 2 * members)
        if paired:
            pass_copy(level, mine, side).start()
        second_filler()

        def hear(k, _):
            peer = exchange(level, k, True)
            whole_copy(level, peer, peer).wait_recv()
            if paired:
                pass_copy(level, peer, side).start()
            return 0

        lax.fori_loop(1, n, hear, 0, unroll=n <= 2 * members)
        inverse = inverses[level]
        width = inverse.shape[1]

        def multiply(i, total, from_side):
            start = (i * step + from_side) * members
            pieces = [whole[base + start + c] for c in range(members)]
            at = pl.ds(pl.multiple_of(start * width, members * width), members * width)
            return total + jnp.dot(
                jnp.concatenate(pieces, axis=1), inverse[at, :], preferred_element_type=jnp.float32
            )

        total = jnp.zeros(out_ref.shape[1:], jnp.float32)
        total = lax.fori_loop(
            0, n // members, lambda i, total: multiply(i, total, side), total
        )
        if paired:

            def passed(k, _):
                pass_copy(level, k, 1 - side).wait_recv()
                return 0

            lax.fori_loop(0, n, passed, 0)
            total = lax.fori_loop(
                0, n // members, lambda i, total: multiply(i, total, 1 - side), total
            )
        value = total.astype(jnp.bfloat16)
        out_ref[level] = value
        return value

    def drain(level):
        _, step, side, mine, n, base = place(level)

        def one(k, _):
            peer = exchange(level, k)
            part_copy(level, peer, mine).wait_send()
            whole_copy(level, peer, mine).wait_send()
            return 0

        lax.fori_loop(1, n, one, 0)
        if step > 1:

            def two(index, _):
                pair_copy(level, index).wait_send()
                pass_copy(level, index, side).wait_send()
                return 0

            lax.fori_loop(0, n, two, 0)

    _, _, side, mine, n, _ = place(LEVELS - 1)
    barrier = pltpu.get_barrier_semaphore()
    pl.semaphore_signal(
        barrier, inc=1, device_id=device(LEVELS - 1, mine, 1 - side), device_id_type=MESH
    )

    def greet(k, _):
        pl.semaphore_signal(
            barrier,
            inc=1,
            device_id=device(LEVELS - 1, exchange(LEVELS - 1, k), side),
            device_id_type=MESH,
        )
        return 0

    lax.fori_loop(1, n, greet, 0)
    loads[0].wait()
    for load in loads[1:]:
        load.start()
    leaf_products(0)

    def ready(q, _):
        sends[q] = leaf_sum(0, q).astype(jnp.bfloat16)
        return 0

    lax.fori_loop(0, members, ready, 0)
    pl.semaphore_wait(barrier, n)

    def base_mid():
        loads[1].wait()
        leaf_products(1)
        leaf_base(1, lambda total, q: total)

    def products_top():
        for load in loads[2:]:
            load.wait()
        leaf_products(2)

    def base_top():
        products(first, 1, 1)
        leaf_base(2, lambda total, q: term_sum(total, 1, 1, q))

    def nothing():
        pass

    first = settle(0, lambda q: leaf_sum(0, q), base_mid, products_top)
    products(first, 0, 0)
    second = settle(1, lambda q: term_sum(base_sums[q], 0, 0, q), base_top, nothing)
    products(second, 2, 2)
    settle(2, lambda q: term_sum(base_sums[2 * members + q], 2, 2, q), nothing, nothing)
    for level in range(LEVELS):
        drain(level)


def on_device(
    leaf_solution,
    leaf_panels,
    leaf_rows,
    sep_panels,
    sep_rows,
    right_sides,
    inverse_low,
    inverse_mid,
    inverse_top,
):
    members = lax.axis_size("member")
    blocks, height, width = leaf_solution.shape
    slots = members * (2**LEVELS - 1)
    vmem = pl.BlockSpec(memory_space=pltpu.VMEM)
    smem = pl.BlockSpec(memory_space=pltpu.SMEM)
    hbm = pl.BlockSpec(memory_space=pl.ANY)
    each = sep_panels.shape[2]
    out = pl.pallas_call(
        functools.partial(solve_kernel, members),
        out_shape=jax.ShapeDtypeStruct((LEVELS, height, width), jnp.bfloat16),
        in_specs=[smem, smem, vmem, vmem, hbm, hbm, hbm, hbm, hbm],
        out_specs=vmem,
        scratch_shapes=[
            pltpu.VMEM((slots - members, height, width), jnp.float32),
            pltpu.VMEM((slots, height, width), jnp.bfloat16),
            pltpu.VMEM((slots, height, width), jnp.bfloat16),
            pltpu.VMEM((slots, height, width), jnp.bfloat16),
            pltpu.VMEM((slots, height, width), jnp.bfloat16),
            pltpu.VMEM((blocks * each, height, width), jnp.float32),
            pltpu.VMEM((LEVELS * each, height, width), jnp.float32),
            pltpu.VMEM((LEVELS, blocks, each, width, width), jnp.bfloat16),
            pltpu.VMEM(sep_panels.shape[1:], jnp.bfloat16),
            pltpu.VMEM(inverse_low.shape[1:], jnp.bfloat16),
            pltpu.VMEM(inverse_mid.shape[1:], jnp.bfloat16),
            pltpu.VMEM(inverse_top.shape[1:], jnp.bfloat16),
            pltpu.SemaphoreType.DMA((LEVELS + 4,)),
            pltpu.SemaphoreType.DMA((slots,)),
            pltpu.SemaphoreType.DMA((slots,)),
            pltpu.SemaphoreType.DMA((slots,)),
            pltpu.SemaphoreType.DMA((slots,)),
            pltpu.SemaphoreType.DMA((slots,)),
            pltpu.SemaphoreType.DMA((slots,)),
            pltpu.SemaphoreType.DMA((slots,)),
        ],
        compiler_params=pltpu.CompilerParams(collective_id=0, has_side_effects=True),
        name="solve",
    )(
        leaf_rows.transpose(1, 2, 0),
        sep_rows.transpose(1, 0, 2),
        leaf_solution,
        right_sides[:, 0],
        leaf_panels,
        sep_panels[0],
        inverse_low[0],
        inverse_mid[0],
        inverse_top[0],
    )
    return out[:, None]


def solution(mesh):
    placed = (
        P(("group", "member"), None, None),
        P(("group", "member"), None, None, None, None),
        P(("group", "member"), None, None),
        P(("group", "member"), None, None, None, None),
        P(("group", "member"), None, None),
        P(None, ("group", "member"), None, None),
        P(("group", "member"), None, None),
        P(("group", "member"), None, None),
        P(("group", "member"), None, None),
    )
    return jax.shard_map(
        on_device,
        mesh=mesh,
        in_specs=placed,
        out_specs=P(None, ("group", "member"), None, None),
        check_vma=False,
    )
```
